32 devices in a mesh: sector: 16 (over z, y, x), op: 2 (over core).
Axes of the slice: x: 2, y: 2, z: 4, core: 2. Of those that a mesh axis runs over, the one named last changes fastest.
Arguments:
- psi: bfloat16 [1024, 128, 128], P('sector'), may hold values from -6 to 6
- left_env: bfloat16 [2, 128, 128, 128], P('op', 'sector'), may hold values from -0.5 to 0.5
- right_env: bfloat16 [2, 128, 128, 128], P('op', 'sector'), may hold values from -0.375 to 0.375
- left_dims: int32 [128], replicated, may hold values from 64 to 128
- right_dims: int32 [128], replicated, may hold values from 64 to 128
- block_right: int32 [1024], replicated, may hold values from 0 to 127, as said below
Outputs:
- h_psi: bfloat16 [1024, 128, 128], P('sector', 'op')
The draws below stay inside these ranges and needn't reach their ends.
Inputs may be any that keep to these rules, and one draw needn't show every extreme that they name: Block d * 64 + j lies in left sector d * 8 + j // 8; its right sector is owned by index block_right // 8 of sector, and block_right % 8 equals j // 8. Of the 64 blocks of each index of sector, exactly 4 have their right sector owned by each index of sector; the 8 blocks of one left sector have distinct right sectors, and every right sector is paired with exactly 8 blocks.
All inputs are finite; a program needn't handle non-finite values.
Results may differ from the reference program's by a relative error of at most 0.0049.
Values may be sent and summed in bfloat16 or wider, within the bound.
A program may use at most 64 MiB of HBM per device.

```python
import jax
import jax.numpy as jnp
from jax import lax

P_SIZE = 128
SEC_DEV = 8
BLK_DEV = 64
NPART = 8
CAP = 4
K = 2
NS = 128
NBLK = 1024


def draw_block_right(key, part):
    device_count = NS // SEC_DEV
    shuffle = jax.random.permutation(jax.random.fold_in(key, 7), device_count).astype(jnp.int32)
    inverse_map = jnp.argsort(shuffle).astype(jnp.int32)
    source = jnp.arange(NBLK, dtype=jnp.int32) // BLK_DEV
    within = jnp.arange(NBLK, dtype=jnp.int32) % BLK_DEV
    offset = within // CAP
    owner = shuffle[(inverse_map[source] + offset) % device_count]
    return (owner * SEC_DEV + within // NPART).astype(jnp.int32)


def set_ends(values, key, low, top_value):
    longest = values.shape.index(max(values.shape))
    spots = []
    for shift in (0, 1):
        where = [jax.random.randint(jax.random.fold_in(key, axis), (), 0, length) for axis, length in enumerate(values.shape)]
        where[longest] = (where[longest] + shift) % values.shape[longest]
        spots.append(tuple(where))
    return values.at[spots[0]].set(low).at[spots[1]].set(top_value)


def steps_of(key, extent, pieces, low, high):
    factor_of, own = 1.0, jax.random.fold_in(key, 6)
    for dim, parts in pieces:
        heights = jnp.exp(jax.random.uniform(jax.random.fold_in(own, dim), (parts,), jnp.float32, low / len(pieces), high / len(pieces)))
        factor_of = factor_of * jnp.repeat(heights, extent[dim] // parts).reshape([-1 if axis == dim else 1 for axis in range(len(extent))])
    return factor_of


def centred(stream_key, shape, deviation, most, cuts=(), held_as=jnp.bfloat16):
    values = deviation * jax.random.normal(stream_key, shape, jnp.float32)
    if cuts:
        values = values * steps_of(stream_key, shape, cuts, -0.22, 0.18)
    return jnp.clip(values, -most, most).astype(held_as)


def setup_inputs(seed: int = 0) -> dict:
    key_of = jax.random.split(jax.random.key(seed), 7)
    return {
        "psi": centred(key_of[0], (NBLK, P_SIZE, P_SIZE), 1.0, 6.0, ((0, 16),)),
        "left_env": centred(key_of[1], (K, NS, P_SIZE, P_SIZE), P_SIZE ** -0.5, 0.5, ((0, 2), (1, 16))),
        "right_env": centred(key_of[2], (K, NS, P_SIZE, P_SIZE), (P_SIZE * K) ** -0.5, 0.375, ((0, 2), (1, 16))),
        "left_dims": set_ends(jax.random.randint(key_of[3], (NS,), P_SIZE // 2, P_SIZE + 1), jax.random.fold_in(key_of[3], 1), P_SIZE // 2, P_SIZE).astype(jnp.int32),
        "right_dims": set_ends(jax.random.randint(key_of[4], (NS,), P_SIZE // 2, P_SIZE + 1), jax.random.fold_in(key_of[4], 1), P_SIZE // 2, P_SIZE).astype(jnp.int32),
        "block_right": draw_block_right(jax.random.fold_in(key_of[6], 71), 0),
    }


def reference(psi, left_env, right_env, left_dims, right_dims, block_right):
    position = jnp.arange(P_SIZE, dtype=jnp.int32)
    by_sector = psi.reshape(NS, NPART, P_SIZE, P_SIZE)
    right_of = block_right.reshape(NS, NPART)

    def one_sector(sector_index):
        row_limit = left_dims[sector_index]
        right_sector = right_of[sector_index]
        col_limit = right_dims[right_sector]
        row_keep = (position < row_limit).astype(jnp.float32)
        col_keep = (position[None, :] < col_limit[:, None]).astype(jnp.float32)
        keep_mask = row_keep[None, :, None] * col_keep[:, None, :]
        masked = by_sector[sector_index].astype(jnp.float32) * keep_mask
        left_block = left_env[:, sector_index].astype(jnp.float32)
        products = jnp.einsum("kab,nbc->knac", left_block, masked)
        products = lax.optimization_barrier(products.astype(jnp.bfloat16)).astype(jnp.float32)
        right_blocks = right_env[:, right_sector].astype(jnp.float32)
        summed = jnp.einsum("knac,kndc->nad", products, right_blocks)
        return (summed * keep_mask).astype(jnp.bfloat16)

    outputs = lax.map(one_sector, jnp.arange(NS, dtype=jnp.int32))
    return outputs.reshape(NBLK, P_SIZE, P_SIZE)
```

```python
import functools

import jax
import jax.numpy as jnp
from jax import lax
from jax.experimental import pallas as pl
from jax.experimental.pallas import tpu as pltpu
from jax.sharding import PartitionSpec as P

MESH = pl.DeviceIdType.MESH

def combine(partial_sum):
    row_count = partial_sum.shape[1] // lax.axis_size("op")
    whole = lax.psum(partial_sum, "op")
    return lax.dynamic_slice_in_dim(whole, lax.axis_index("op") * row_count, row_count, 1)


def exchange_path(psi, left_env, right_env, left_dims, right_dims, block_right):
    devices = lax.axis_size("sector")
    sector_index = lax.axis_index("sector")
    blocks = psi.shape[0]
    block_width = psi.shape[1]
    term_count = left_env.shape[0]
    sectors = left_env.shape[1]
    coupled = blocks // sectors
    slot_count = blocks // devices
    counter = jnp.arange(blocks, dtype=jnp.int32)
    mine_right = lax.dynamic_slice_in_dim(block_right, sector_index * blocks, blocks)
    mine_owner = mine_right // sectors
    send_order = jnp.argsort(mine_owner * blocks + counter)
    inverse = jnp.argsort(send_order)
    own_dims = lax.dynamic_slice_in_dim(left_dims, sector_index * sectors, sectors)
    row_limit = jnp.repeat(own_dims, coupled)
    col_limit = right_dims[mine_right]
    position = jnp.arange(block_width, dtype=jnp.int32)
    keep_mask = (position[None, :, None] < row_limit[:, None, None]) & (
        position[None, None, :] < col_limit[:, None, None]
    )
    masked = psi * keep_mask.astype(psi.dtype)
    products = jnp.einsum(
        "ksab,snbc->ksnac",
        left_env,
        masked.reshape(sectors, coupled, block_width, block_width),
        preferred_element_type=jnp.float32,
    )
    products = products.astype(jnp.bfloat16).reshape(term_count, blocks, block_width, block_width)
    owners_all = (block_right // sectors).reshape(devices, blocks)
    foreign = (owners_all != sector_index).astype(jnp.int32)
    incoming = jnp.argsort(foreign * blocks + counter[None, :], axis=1)[:, :slot_count]
    arriving = (
        jnp.take_along_axis(block_right.reshape(devices, blocks), incoming, axis=1).reshape(-1)
        - sector_index * sectors
    )
    outgoing = right_env[:, arriving].reshape(
        term_count, devices, slot_count, block_width, block_width
    )
    received = lax.all_to_all(outgoing, "sector", split_axis=1, concat_axis=1, tiled=True)
    chosen = received.reshape(term_count, blocks, block_width, block_width)[:, inverse]
    partial_sum = jnp.einsum("kjab,kjcb->jac", products, chosen, preferred_element_type=jnp.float32)
    result = combine(partial_sum).astype(jnp.bfloat16)
    row_count = result.shape[1]
    op_index = lax.axis_index("op")
    row_position = op_index * row_count + jnp.arange(row_count, dtype=jnp.int32)
    keep_rows = (row_position[None, :, None] < row_limit[:, None, None]) & (
        position[None, None, :] < col_limit[:, None, None]
    )
    return result * keep_rows.astype(jnp.bfloat16)


def gather_kernel(
    devices, block_right, left_dims, right_dims, rank, source, psi_hbm, left_hbm, right_hbm, out,
    psi, left, products, full, stage, got, part, partner_part,
    local_sem, own_sem, z_send, z_recv, n_send, n_recv, s_send, s_recv, p_send, p_recv,
):
    me = lax.axis_index("sector")
    core = lax.axis_index("op")
    depth = devices // 4
    z, y, x = me // 4, (me // 2) % 2, me % 2
    x_mate, y_mate = me + 1 - 2 * x, me + 2 - 4 * y
    blocks, width = psi.shape[0], psi.shape[1]
    sectors = left.shape[0]
    coupled = blocks // sectors
    slots = blocks // devices
    half = width // 2
    place = (y, x)
    near = (y_mate, x_mate)
    far = (x_mate, y_mate)

    own = [
        pltpu.make_async_copy(
            right_hbm.at[0, :, pl.ds(h * half, half), :], full.at[h, z, place[h]], own_sem.at[h]
        )
        for h in (0, 1)
    ]
    load_left = pltpu.make_async_copy(left_hbm.at[0], left, local_sem.at[0])
    load_psi = pltpu.make_async_copy(psi_hbm, psi, local_sem.at[1])
    for copy in (*own, load_left, load_psi):
        copy.start()

    barrier = pltpu.get_barrier_semaphore()
    for mate in (x_mate, y_mate):
        pl.semaphore_signal(barrier, inc=1, device_id={"sector": mate}, device_id_type=MESH)
    pl.semaphore_signal(barrier, inc=1, device_id={"op": 1 - core}, device_id_type=MESH)

    @pl.when(z > 0)
    def _():
        pl.semaphore_signal(barrier, inc=1, device_id={"sector": me - 4}, device_id_type=MESH)

    @pl.when(z < depth - 1)
    def _():
        pl.semaphore_signal(barrier, inc=1, device_id={"sector": me + 4}, device_id_type=MESH)

    pl.semaphore_wait(barrier, 3 + (z > 0).astype(jnp.int32) + (z < depth - 1).astype(jnp.int32))
    for copy in own:
        copy.wait()

    def remote(src, dst, send, recv, target):
        return pltpu.make_async_remote_copy(
            src_ref=src, dst_ref=dst, send_sem=send, recv_sem=recv, device_id=target, device_id_type=MESH
        )

    def along_z(h, zz, up):
        block = full.at[h, zz, place[h]]
        target = {"sector": me + 4 if up else me - 4}
        return remote(block, block, z_send.at[h, zz, int(up)], z_recv.at[h, zz], target)

    def to_near(h, zz):
        block = full.at[h, zz, place[h]]
        return remote(block, block, n_send.at[h, zz], n_recv.at[h, zz], {"sector": near[h]})

    def to_far(h, zz, p):
        return remote(
            stage.at[h, zz, p], got.at[h, zz, p], s_send.at[h, zz, p], s_recv.at[h, zz, p], {"sector": far[h]}
        )

    def select_and_send(h, zz, p):
        owner = (zz * 2 + p) * 2 + x if h == 0 else (zz * 2 + y) * 2 + p
        for t in range(slots):
            wanted = source[(h * devices + owner) * slots + t]
            value = full[h, zz, p, 0]
            for s in range(1, sectors):
                value = jnp.where(wanted == s, full[h, zz, p, s], value)
            stage[h, zz, p, t] = value
        to_far(h, zz, p).start()

    def arrived(zz, ups):
        for h in (0, 1):
            for up in ups:
                @pl.when(z < depth - 1 if up else z > 0)
                def _():
                    along_z(h, zz, up).start()
            to_near(h, zz).start()
        for h in (0, 1):
            select_and_send(h, zz, place[h])

    def near_arrived(zz):
        for h in (0, 1):
            to_near(h, zz).wait_recv()
            select_and_send(h, zz, 1 - place[h])

    columns = lax.broadcasted_iota(jnp.int32, (width, width), 1)

    def multiply_left(s, _):
        row_limit = left_dims[me * sectors + s]
        env = jnp.where(columns < row_limit, left[s].astype(jnp.float32), 0.0).astype(jnp.bfloat16)
        for n in range(coupled):
            j = s * coupled + n
            col_limit = right_dims[block_right[me * blocks + j]]
            value = jnp.dot(env, psi[j], preferred_element_type=jnp.float32)
            products[j] = jnp.where(columns < col_limit, value, 0.0).astype(jnp.bfloat16)
        return 0

    arrived(z, (False, True))
    load_left.wait()
    load_psi.wait()
    lax.fori_loop(0, sectors // 2, multiply_left, 0)
    near_arrived(z)
    for step in range(1, depth):
        below, above = z - step, z + step

        def enter(zz, up):
            for h in (0, 1):
                along_z(h, zz, up).wait_recv()
            arrived(zz, (up,))

        pl.when(below >= 0)(functools.partial(enter, below, True))
        pl.when(above < depth)(functools.partial(enter, above, False))
        if step == 1:
            lax.fori_loop(sectors // 2, sectors, multiply_left, 0)
        pl.when(below >= 0)(functools.partial(near_arrived, below))
        pl.when(above < depth)(functools.partial(near_arrived, above))
    for h in (0, 1):
        for zz in range(depth):
            for p in (0, 1):
                to_far(h, zz, p).wait_recv()

    def swap(s):
        span = pl.ds(s * coupled, coupled)
        return remote(
            part.at[1 - core, span], partner_part.at[span], p_send.at[s], p_recv.at[s], {"op": 1 - core}
        )

    def multiply_right(s, _):
        for n in range(coupled):
            j = s * coupled + n
            owner = block_right[me * blocks + j] // sectors
            oz, oy, ox = owner // 4, (owner // 2) % 2, owner % 2
            slot = rank[j]
            top = jnp.where(ox == x, full[0, oz, oy, s], got[0, oz, oy, slot])
            low = jnp.where(oy == y, full[1, oz, ox, s], got[1, oz, ox, slot])
            env = jnp.concatenate([top, low], axis=0)
            value = lax.dot_general(
                products[j], env, (((1,), (1,)), ((), ())), preferred_element_type=jnp.float32
            )
            part[0, j] = value[:half].astype(part.dtype)
            part[1, j] = value[half:].astype(part.dtype)
        swap(s).start()
        return 0

    def finish(s):
        swap(s).wait_recv()
        rows = lax.broadcasted_iota(jnp.int32, (half, width), 0) + core * half
        row_limit = left_dims[me * sectors + s]
        for n in range(coupled):
            j = s * coupled + n
            col_limit = right_dims[block_right[me * blocks + j]]
            value = part[core, j].astype(jnp.float32) + partner_part[j].astype(jnp.float32)
            keep = (rows < row_limit) & (columns[:half] < col_limit)
            out[j] = jnp.where(keep, value, 0.0).astype(jnp.bfloat16)

    lag = 2
    lax.fori_loop(0, lag, multiply_right, 0)

    def both(s, _):
        multiply_right(s, 0)
        finish(s - lag)
        return 0

    lax.fori_loop(lag, sectors, both, 0)

    def last(s, _):
        finish(s)
        return 0

    lax.fori_loop(sectors - lag, sectors, last, 0)

    def drain(s, _):
        swap(s).wait_send()
        return 0

    lax.fori_loop(0, sectors, drain, 0)
    for h in (0, 1):
        for zz in range(depth):
            to_near(h, zz).wait_send()
            for p in (0, 1):
                to_far(h, zz, p).wait_send()
            pl.when((z > 0) & (z <= zz))(lambda: along_z(h, zz, False).wait_send())
            pl.when((z < depth - 1) & (z >= zz))(lambda: along_z(h, zz, True).wait_send())


def tables(block_right, devices, blocks, sectors):
    me = lax.axis_index("sector")
    slots = blocks // devices
    members = jnp.stack([me, me ^ 1, me ^ 2])
    owners = (block_right.reshape(devices, blocks) // sectors)[members]
    position = jnp.arange(blocks, dtype=jnp.int32)
    earlier = (owners[:, None, :] == owners[:, :, None]) & (position[None, None, :] < position[None, :, None])
    rank = jnp.sum(earlier.astype(jnp.int32), axis=2)
    code = owners[1:] * slots + rank[1:]
    hit = code[:, None, :] == jnp.arange(devices * slots, dtype=jnp.int32)[None, :, None]
    source = jnp.sum(hit * (position // (blocks // sectors)), axis=2)
    return rank[0], source.reshape(-1)


def per_device(psi, left_env, right_env, left_dims, right_dims, block_right):
    devices, cores = lax.axis_size("sector"), lax.axis_size("op")
    blocks, width = psi.shape[0], psi.shape[1]
    terms, sectors = left_env.shape[0], left_env.shape[1]
    if cores != 2 or devices % 4 or terms != 1 or blocks % devices or blocks // devices > sectors:
        return exchange_path(psi, left_env, right_env, left_dims, right_dims, block_right)
    depth, half, slots = devices // 4, width // 2, blocks // devices
    rank, source = tables(block_right, devices, blocks, sectors)
    smem, anywhere = pl.BlockSpec(memory_space=pltpu.SMEM), pl.BlockSpec(memory_space=pl.ANY)
    dma, bf16 = pltpu.SemaphoreType.DMA, jnp.bfloat16
    return pl.pallas_call(
        functools.partial(gather_kernel, devices),
        out_shape=jax.ShapeDtypeStruct((blocks, half, width), bf16),
        in_specs=[smem] * 5 + [anywhere] * 3,
        out_specs=pl.BlockSpec(memory_space=pltpu.VMEM),
        scratch_shapes=[
            pltpu.VMEM((blocks, width, width), bf16),
            pltpu.VMEM((sectors, width, width), bf16),
            pltpu.VMEM((blocks, width, width), bf16),
            pltpu.VMEM((2, depth, 2, sectors, half, width), bf16),
            pltpu.VMEM((2, depth, 2, slots, half, width), bf16),
            pltpu.VMEM((2, depth, 2, slots, half, width), bf16),
            pltpu.VMEM((2, blocks, half, width), jnp.float32),
            pltpu.VMEM((blocks, half, width), jnp.float32),
            dma((2,)),
            dma((2,)),
            dma((2, depth, 2)),
            dma((2, depth)),
            dma((2, depth)),
            dma((2, depth)),
            dma((2, depth, 2)),
            dma((2, depth, 2)),
            dma((sectors,)),
            dma((sectors,)),
        ],
        compiler_params=pltpu.CompilerParams(collective_id=0, has_side_effects=True),
    )(block_right, left_dims, right_dims, rank, source, psi, left_env, right_env)


def solution(mesh):
    in_specs = (
        P("sector", None, None),
        P("op", "sector", None, None),
        P("op", "sector", None, None),
        P(),
        P(),
        P(),
    )
    out_specs = P("sector", "op", None)
    return jax.shard_map(
        per_device, mesh=mesh, in_specs=in_specs, out_specs=out_specs, check_vma=False
    )
```

```python
import functools

import jax
import jax.numpy as jnp
from jax import lax
from jax.experimental import pallas as pl
from jax.experimental.pallas import tpu as pltpu
from jax.sharding import PartitionSpec as P

MESH = pl.DeviceIdType.MESH

def combine(partial_sum):
    row_count = partial_sum.shape[1] // lax.axis_size("op")
    whole = lax.psum(partial_sum, "op")
    return lax.dynamic_slice_in_dim(whole, lax.axis_index("op") * row_count, row_count, 1)


def exchange_path(psi, left_env, right_env, left_dims, right_dims, block_right):
    devices = lax.axis_size("sector")
    sector_index = lax.axis_index("sector")
    blocks = psi.shape[0]
    block_width = psi.shape[1]
    term_count = left_env.shape[0]
    sectors = left_env.shape[1]
    coupled = blocks // sectors
    slot_count = blocks // devices
    counter = jnp.arange(blocks, dtype=jnp.int32)
    mine_right = lax.dynamic_slice_in_dim(block_right, sector_index * blocks, blocks)
    mine_owner = mine_right // sectors
    send_order = jnp.argsort(mine_owner * blocks + counter)
    inverse = jnp.argsort(send_order)
    own_dims = lax.dynamic_slice_in_dim(left_dims, sector_index * sectors, sectors)
    row_limit = jnp.repeat(own_dims, coupled)
    col_limit = right_dims[mine_right]
    position = jnp.arange(block_width, dtype=jnp.int32)
    keep_mask = (position[None, :, None] < row_limit[:, None, None]) & (
        position[None, None, :] < col_limit[:, None, None]
    )
    masked = psi * keep_mask.astype(psi.dtype)
    products = jnp.einsum(
        "ksab,snbc->ksnac",
        left_env,
        masked.reshape(sectors, coupled, block_width, block_width),
        preferred_element_type=jnp.float32,
    )
    products = products.astype(jnp.bfloat16).reshape(term_count, blocks, block_width, block_width)
    owners_all = (block_right // sectors).reshape(devices, blocks)
    foreign = (owners_all != sector_index).astype(jnp.int32)
    incoming = jnp.argsort(foreign * blocks + counter[None, :], axis=1)[:, :slot_count]
    arriving = (
        jnp.take_along_axis(block_right.reshape(devices, blocks), incoming, axis=1).reshape(-1)
        - sector_index * sectors
    )
    outgoing = right_env[:, arriving].reshape(
        term_count, devices, slot_count, block_width, block_width
    )
    received = lax.all_to_all(outgoing, "sector", split_axis=1, concat_axis=1, tiled=True)
    chosen = received.reshape(term_count, blocks, block_width, block_width)[:, inverse]
    partial_sum = jnp.einsum("kjab,kjcb->jac", products, chosen, preferred_element_type=jnp.float32)
    result = combine(partial_sum).astype(jnp.bfloat16)
    row_count = result.shape[1]
    op_index = lax.axis_index("op")
    row_position = op_index * row_count + jnp.arange(row_count, dtype=jnp.int32)
    keep_rows = (row_position[None, :, None] < row_limit[:, None, None]) & (
        position[None, None, :] < col_limit[:, None, None]
    )
    return result * keep_rows.astype(jnp.bfloat16)


def gather_kernel(
    devices, block_right, left_dims, right_dims, rank, source, psi_hbm, left_hbm, right_hbm, out,
    psi, left, products, full, stage, got, part, partner_part,
    local_sem, own_sem, z_send, z_recv, n_send, n_recv, s_send, s_recv, p_send, p_recv,
):
    me = lax.axis_index("sector")
    core = lax.axis_index("op")
    depth = devices // 4
    z, y, x = me // 4, (me // 2) % 2, me % 2
    x_mate, y_mate = me + 1 - 2 * x, me + 2 - 4 * y
    blocks, width = psi.shape[0], psi.shape[1]
    sectors = left.shape[0]
    coupled = blocks // sectors
    slots = blocks // devices
    half = width // 2
    place = (y, x)
    near = (y_mate, x_mate)
    far = (x_mate, y_mate)

    own = [
        pltpu.make_async_copy(
            right_hbm.at[0, :, pl.ds(h * half, half), :], full.at[h, z, place[h]], own_sem.at[h]
        )
        for h in (0, 1)
    ]
    load_left = pltpu.make_async_copy(left_hbm.at[0], left, local_sem.at[0])
    load_psi = pltpu.make_async_copy(psi_hbm, psi, local_sem.at[1])
    for copy in (*own, load_left, load_psi):
        copy.start()

    barrier = pltpu.get_barrier_semaphore()
    for mate in (x_mate, y_mate):
        pl.semaphore_signal(barrier, inc=1, device_id={"sector": mate}, device_id_type=MESH)
    pl.semaphore_signal(barrier, inc=1, device_id={"op": 1 - core}, device_id_type=MESH)

    @pl.when(z > 0)
    def _():
        pl.semaphore_signal(barrier, inc=1, device_id={"sector": me - 4}, device_id_type=MESH)

    @pl.when(z < depth - 1)
    def _():
        pl.semaphore_signal(barrier, inc=1, device_id={"sector": me + 4}, device_id_type=MESH)

    pl.semaphore_wait(barrier, 3 + (z > 0).astype(jnp.int32) + (z < depth - 1).astype(jnp.int32))
    for copy in own:
        copy.wait()

    def remote(src, dst, send, recv, target):
        return pltpu.make_async_remote_copy(
            src_ref=src, dst_ref=dst, send_sem=send, recv_sem=recv, device_id=target, device_id_type=MESH
        )

    def along_z(h, zz, up):
        block = full.at[h, zz, place[h]]
        target = {"sector": me + 4 if up else me - 4}
        return remote(block, block, z_send.at[h, zz, int(up)], z_recv.at[h, zz], target)

    def to_near(h, zz):
        block = full.at[h, zz, place[h]]
        return remote(block, block, n_send.at[h, zz], n_recv.at[h, zz], {"sector": near[h]})

    def to_far(h, zz, p):
        return remote(
            stage.at[h, zz, p], got.at[h, zz, p], s_send.at[h, zz, p], s_recv.at[h, zz, p], {"sector": far[h]}
        )

    def select_and_send(h, zz, p):
        owner = (zz * 2 + p) * 2 + x if h == 0 else (zz * 2 + y) * 2 + p
        for t in range(slots):
            wanted = source[far[h], owner * slots + t] // coupled
            value = full[h, zz, p, 0]
            for s in range(1, sectors):
                value = jnp.where(wanted == s, full[h, zz, p, s], value)
            stage[h, zz, p, t] = value
        to_far(h, zz, p).start()

    def arrived(zz, ups):
        for h in (0, 1):
            for up in ups:
                @pl.when(z < depth - 1 if up else z > 0)
                def _():
                    along_z(h, zz, up).start()
            to_near(h, zz).start()
        for h in (0, 1):
            select_and_send(h, zz, place[h])

    def near_arrived(zz):
        for h in (0, 1):
            to_near(h, zz).wait_recv()
            select_and_send(h, zz, 1 - place[h])

    columns = lax.broadcasted_iota(jnp.int32, (width, width), 1)

    def multiply_left(s, _):
        row_limit = left_dims[me * sectors + s]
        env = jnp.where(columns < row_limit, left[s].astype(jnp.float32), 0.0).astype(jnp.bfloat16)
        for n in range(coupled):
            j = s * coupled + n
            col_limit = right_dims[block_right[me * blocks + j]]
            value = jnp.dot(env, psi[j], preferred_element_type=jnp.float32)
            products[j] = jnp.where(columns < col_limit, value, 0.0).astype(jnp.bfloat16)
        return 0

    def swap(zz):
        return remote(
            part.at[1 - core, zz], partner_part.at[zz], p_send.at[zz], p_recv.at[zz], {"op": 1 - core}
        )

    def pick(h, zz, p, wanted):
        value = full[h, zz, p, 0]
        for s in range(1, sectors):
            value = jnp.where(wanted == s, full[h, zz, p, s], value)
        return value

    def multiply_right(zz):
        for h in (0, 1):
            for p in (0, 1):
                to_far(h, zz, p).wait_recv()

        def one(i, _):
            oy, ox, slot = i // (2 * slots), (i // slots) % 2, i % slots
            j = source[me, (zz * 4 + oy * 2 + ox) * slots + slot]
            wanted = j // coupled
            top = jnp.where(ox == x, pick(0, zz, oy, wanted), got[0, zz, oy, slot])
            low = jnp.where(oy == y, pick(1, zz, ox, wanted), got[1, zz, ox, slot])
            env = jnp.concatenate([top, low], axis=0)
            value = lax.dot_general(
                products[j], env, (((1,), (1,)), ((), ())), preferred_element_type=jnp.float32
            )
            part[0, zz, i] = value[:half]
            part[1, zz, i] = value[half:]
            return 0

        lax.fori_loop(0, 4 * slots, one, 0, unroll=4)
        swap(zz).start()

    arrived(z, (False, True))
    load_left.wait()
    load_psi.wait()
    lax.fori_loop(0, sectors // 2, multiply_left, 0)
    near_arrived(z)
    for step in range(1, depth):
        below, above = z - step, z + step

        def enter(zz, up):
            for h in (0, 1):
                along_z(h, zz, up).wait_recv()
            arrived(zz, (up,))

        pl.when(below >= 0)(functools.partial(enter, below, True))
        pl.when(above < depth)(functools.partial(enter, above, False))
        if step == 1:
            lax.fori_loop(sectors // 2, sectors, multiply_left, 0)
        pl.when(below >= 0)(functools.partial(near_arrived, below))
        pl.when(above < depth)(functools.partial(near_arrived, above))
        if step == 1:
            multiply_right(z)
        else:
            pl.when(below + 1 >= 0)(functools.partial(multiply_right, below + 1))
            pl.when(above - 1 < depth)(functools.partial(multiply_right, above - 1))
    pl.when(z - depth + 1 >= 0)(functools.partial(multiply_right, z - depth + 1))
    pl.when(z + depth - 1 < depth)(functools.partial(multiply_right, z + depth - 1))
    def finish(s, _):
        rows = lax.broadcasted_iota(jnp.int32, (half, width), 0) + core * half
        row_limit = left_dims[me * sectors + s]
        for n in range(coupled):
            j = s * coupled + n
            right = block_right[me * blocks + j]
            owner = right // sectors
            oz, i = owner // 4, (owner % 4) * slots + rank[me, j]
            value = part[core, oz, i] + partner_part[oz, i]
            keep = (rows < row_limit) & (columns[:half] < right_dims[right])
            out[j] = jnp.where(keep, value, 0.0).astype(jnp.bfloat16)
        return 0

    for zz in range(depth):
        swap(zz).wait_recv()
    lax.fori_loop(0, sectors, finish, 0)
    for zz in range(depth):
        swap(zz).wait_send()
    for h in (0, 1):
        for zz in range(depth):
            to_near(h, zz).wait_send()
            for p in (0, 1):
                to_far(h, zz, p).wait_send()
            pl.when((z > 0) & (z <= zz))(lambda: along_z(h, zz, False).wait_send())
            pl.when((z < depth - 1) & (z >= zz))(lambda: along_z(h, zz, True).wait_send())


def tables(block_right, devices, blocks, sectors):
    slots = blocks // devices
    owners = (block_right // sectors).reshape(devices, blocks)
    position = jnp.arange(blocks, dtype=jnp.int32)
    earlier = (owners[:, None, :] == owners[:, :, None]) & (position[None, None, :] < position[None, :, None])
    rank = jnp.sum(earlier.astype(jnp.int32), axis=2)
    code = owners * slots + rank
    hit = code[:, None, :] == jnp.arange(devices * slots, dtype=jnp.int32)[None, :, None]
    source = jnp.sum(jnp.where(hit, position, 0), axis=2)
    return rank, source


def per_device(psi, left_env, right_env, left_dims, right_dims, block_right):
    devices, cores = lax.axis_size("sector"), lax.axis_size("op")
    blocks, width = psi.shape[0], psi.shape[1]
    terms, sectors = left_env.shape[0], left_env.shape[1]
    if cores != 2 or devices % 4 or terms != 1 or blocks % devices or blocks // devices > sectors:
        return exchange_path(psi, left_env, right_env, left_dims, right_dims, block_right)
    depth, half, slots = devices // 4, width // 2, blocks // devices
    rank, source = tables(block_right, devices, blocks, sectors)
    smem, anywhere = pl.BlockSpec(memory_space=pltpu.SMEM), pl.BlockSpec(memory_space=pl.ANY)
    dma, bf16 = pltpu.SemaphoreType.DMA, jnp.bfloat16
    return pl.pallas_call(
        functools.partial(gather_kernel, devices),
        out_shape=jax.ShapeDtypeStruct((blocks, half, width), bf16),
        in_specs=[smem] * 5 + [anywhere] * 3,
        out_specs=pl.BlockSpec(memory_space=pltpu.VMEM),
        scratch_shapes=[
            pltpu.VMEM((blocks, width, width), bf16),
            pltpu.VMEM((sectors, width, width), bf16),
            pltpu.VMEM((blocks, width, width), bf16),
            pltpu.VMEM((2, depth, 2, sectors, half, width), bf16),
            pltpu.VMEM((2, depth, 2, slots, half, width), bf16),
            pltpu.VMEM((2, depth, 2, slots, half, width), bf16),
            pltpu.VMEM((2, depth, 4 * slots, half, width), jnp.float32),
            pltpu.VMEM((depth, 4 * slots, half, width), jnp.float32),
            dma((2,)),
            dma((2,)),
            dma((2, depth, 2)),
            dma((2, depth)),
            dma((2, depth)),
            dma((2, depth)),
            dma((2, depth, 2)),
            dma((2, depth, 2)),
            dma((depth,)),
            dma((depth,)),
        ],
        compiler_params=pltpu.CompilerParams(collective_id=0, has_side_effects=True),
    )(block_right, left_dims, right_dims, rank, source, psi, left_env, right_env)


def solution(mesh):
    in_specs = (
        P("sector", None, None),
        P("op", "sector", None, None),
        P("op", "sector", None, None),
        P(),
        P(),
        P(),
    )
    out_specs = P("sector", "op", None)
    return jax.shard_map(
        per_device, mesh=mesh, in_specs=in_specs, out_specs=out_specs, check_vma=False
    )
```

```python
import functools

import jax
import jax.numpy as jnp
from jax import lax
from jax.experimental import pallas as pl
from jax.experimental.pallas import tpu as pltpu
from jax.sharding import PartitionSpec as P

MESH = pl.DeviceIdType.MESH

def combine(partial_sum):
    row_count = partial_sum.shape[1] // lax.axis_size("op")
    whole = lax.psum(partial_sum, "op")
    return lax.dynamic_slice_in_dim(whole, lax.axis_index("op") * row_count, row_count, 1)


def exchange_path(psi, left_env, right_env, left_dims, right_dims, block_right):
    devices = lax.axis_size("sector")
    sector_index = lax.axis_index("sector")
    blocks = psi.shape[0]
    block_width = psi.shape[1]
    term_count = left_env.shape[0]
    sectors = left_env.shape[1]
    coupled = blocks // sectors
    slot_count = blocks // devices
    counter = jnp.arange(blocks, dtype=jnp.int32)
    mine_right = lax.dynamic_slice_in_dim(block_right, sector_index * blocks, blocks)
    mine_owner = mine_right // sectors
    send_order = jnp.argsort(mine_owner * blocks + counter)
    inverse = jnp.argsort(send_order)
    own_dims = lax.dynamic_slice_in_dim(left_dims, sector_index * sectors, sectors)
    row_limit = jnp.repeat(own_dims, coupled)
    col_limit = right_dims[mine_right]
    position = jnp.arange(block_width, dtype=jnp.int32)
    keep_mask = (position[None, :, None] < row_limit[:, None, None]) & (
        position[None, None, :] < col_limit[:, None, None]
    )
    masked = psi * keep_mask.astype(psi.dtype)
    products = jnp.einsum(
        "ksab,snbc->ksnac",
        left_env,
        masked.reshape(sectors, coupled, block_width, block_width),
        preferred_element_type=jnp.float32,
    )
    products = products.astype(jnp.bfloat16).reshape(term_count, blocks, block_width, block_width)
    owners_all = (block_right // sectors).reshape(devices, blocks)
    foreign = (owners_all != sector_index).astype(jnp.int32)
    incoming = jnp.argsort(foreign * blocks + counter[None, :], axis=1)[:, :slot_count]
    arriving = (
        jnp.take_along_axis(block_right.reshape(devices, blocks), incoming, axis=1).reshape(-1)
        - sector_index * sectors
    )
    outgoing = right_env[:, arriving].reshape(
        term_count, devices, slot_count, block_width, block_width
    )
    received = lax.all_to_all(outgoing, "sector", split_axis=1, concat_axis=1, tiled=True)
    chosen = received.reshape(term_count, blocks, block_width, block_width)[:, inverse]
    partial_sum = jnp.einsum("kjab,kjcb->jac", products, chosen, preferred_element_type=jnp.float32)
    result = combine(partial_sum).astype(jnp.bfloat16)
    row_count = result.shape[1]
    op_index = lax.axis_index("op")
    row_position = op_index * row_count + jnp.arange(row_count, dtype=jnp.int32)
    keep_rows = (row_position[None, :, None] < row_limit[:, None, None]) & (
        position[None, None, :] < col_limit[:, None, None]
    )
    return result * keep_rows.astype(jnp.bfloat16)


def gather_kernel(
    devices, block_right, left_dims, right_dims, rank, source, psi_hbm, left_hbm, right_hbm, out_hbm,
    out, out_sem, psi, left, products, full, stage, got, part, partner_part,
    local_sem, own_sem, z_send, z_recv, n_send, n_recv, s_send, s_recv, p_send, p_recv,
):
    me = lax.axis_index("sector")
    core = lax.axis_index("op")
    depth = devices // 4
    z, y, x = me // 4, (me // 2) % 2, me % 2
    x_mate, y_mate = me + 1 - 2 * x, me + 2 - 4 * y
    blocks, width = psi.shape[0], psi.shape[1]
    sectors = left.shape[0]
    coupled = blocks // sectors
    slots = blocks // devices
    half = width // 2
    place = (y, x)
    near = (y_mate, x_mate)
    far = (x_mate, y_mate)

    own = [
        pltpu.make_async_copy(
            right_hbm.at[0, :, pl.ds(h * half, half), :], full.at[h, z, place[h]], own_sem.at[h]
        )
        for h in (0, 1)
    ]
    load_left = pltpu.make_async_copy(left_hbm.at[0], left, local_sem.at[0])
    load_psi = pltpu.make_async_copy(psi_hbm, psi, local_sem.at[1])
    for copy in (*own, load_left, load_psi):
        copy.start()

    barrier = pltpu.get_barrier_semaphore()
    for mate in (x_mate, y_mate):
        pl.semaphore_signal(barrier, inc=1, device_id={"sector": mate}, device_id_type=MESH)
    pl.semaphore_signal(barrier, inc=1, device_id={"op": 1 - core}, device_id_type=MESH)

    @pl.when(z > 0)
    def _():
        pl.semaphore_signal(barrier, inc=1, device_id={"sector": me - 4}, device_id_type=MESH)

    @pl.when(z < depth - 1)
    def _():
        pl.semaphore_signal(barrier, inc=1, device_id={"sector": me + 4}, device_id_type=MESH)

    pl.semaphore_wait(barrier, 3 + (z > 0).astype(jnp.int32) + (z < depth - 1).astype(jnp.int32))
    for copy in own:
        copy.wait()

    def remote(src, dst, send, recv, target):
        return pltpu.make_async_remote_copy(
            src_ref=src, dst_ref=dst, send_sem=send, recv_sem=recv, device_id=target, device_id_type=MESH
        )

    pieces = z_recv.shape[2]
    piece = sectors // pieces

    def along_z(h, zz, q, up):
        block = full.at[h, zz, place[h], pl.ds(q * piece, piece)]
        target = {"sector": me + 4 if up else me - 4}
        return remote(block, block, z_send.at[h, zz, q, int(up)], z_recv.at[h, zz, q], target)

    def to_near(h, zz, q):
        block = full.at[h, zz, place[h], pl.ds(q * piece, piece)]
        return remote(block, block, n_send.at[h, zz, q], n_recv.at[h, zz, q], {"sector": near[h]})

    def to_far(h, zz, p):
        return remote(
            stage.at[h, zz, p], got.at[h, zz, p], s_send.at[h, zz, p], s_recv.at[h, zz, p], {"sector": far[h]}
        )

    def select_and_send(h, zz, p):
        owner = (zz * 2 + p) * 2 + x if h == 0 else (zz * 2 + y) * 2 + p
        for t in range(slots):
            wanted = source[far[h], owner * slots + t] // coupled
            value = full[h, zz, p, 0]
            for s in range(1, sectors):
                value = jnp.where(wanted == s, full[h, zz, p, s], value)
            stage[h, zz, p, t] = value
        to_far(h, zz, p).start()

    def arrived(zz, ups, wait):
        for h in (0, 1):
            for q in range(pieces):
                if wait:
                    along_z(h, zz, q, ups[0]).wait_recv()
                for up in ups:
                    @pl.when(z < depth - 1 if up else z > 0)
                    def _():
                        along_z(h, zz, q, up).start()
                to_near(h, zz, q).start()
            if wait:
                select_and_send(h, zz, place[h])
        if not wait:
            for h in (0, 1):
                select_and_send(h, zz, place[h])

    def near_arrived(zz):
        for h in (0, 1):
            for q in range(pieces):
                to_near(h, zz, q).wait_recv()
            select_and_send(h, zz, 1 - place[h])

    columns = lax.broadcasted_iota(jnp.int32, (width, width), 1)

    def multiply_left(s, _):
        row_limit = left_dims[me * sectors + s]
        env = jnp.where(columns < row_limit, left[s].astype(jnp.float32), 0.0).astype(jnp.bfloat16)
        for n in range(coupled):
            j = s * coupled + n
            col_limit = right_dims[block_right[me * blocks + j]]
            value = jnp.dot(env, psi[j], preferred_element_type=jnp.float32)
            products[j] = jnp.where(columns < col_limit, value, 0.0).astype(jnp.bfloat16)
        return 0

    def swap(zz):
        return remote(
            part.at[1 - core, zz], partner_part.at[zz], p_send.at[zz], p_recv.at[zz], {"op": 1 - core}
        )

    def pick(h, zz, p, wanted):
        value = full[h, zz, p, 0]
        for s in range(1, sectors):
            value = jnp.where(wanted == s, full[h, zz, p, s], value)
        return value

    def multiply_right(zz):
        for h in (0, 1):
            for p in (0, 1):
                to_far(h, zz, p).wait_recv()

        def one(i, _):
            oy, ox, slot = i // (2 * slots), (i // slots) % 2, i % slots
            j = source[me, (zz * 4 + oy * 2 + ox) * slots + slot]
            wanted = j // coupled
            top = jnp.where(ox == x, pick(0, zz, oy, wanted), got[0, zz, oy, slot])
            low = jnp.where(oy == y, pick(1, zz, ox, wanted), got[1, zz, ox, slot])
            env = jnp.concatenate([top, low], axis=0)
            value = lax.dot_general(
                products[j], env, (((1,), (1,)), ((), ())), preferred_element_type=jnp.float32
            )
            part[0, zz, i] = value[:half]
            part[1, zz, i] = value[half:]
            return 0

        lax.fori_loop(0, 4 * slots, one, 0, unroll=4)
        swap(zz).start()

    arrived(z, (False, True), False)
    load_left.wait()
    load_psi.wait()
    lax.fori_loop(0, sectors // 2, multiply_left, 0)
    near_arrived(z)
    for step in range(1, depth):
        below, above = z - step, z + step

        def enter(zz, up):
            arrived(zz, (up,), True)

        pl.when(below >= 0)(functools.partial(enter, below, True))
        pl.when(above < depth)(functools.partial(enter, above, False))
        if step == 1:
            lax.fori_loop(sectors // 2, sectors, multiply_left, 0)
        pl.when(below >= 0)(functools.partial(near_arrived, below))
        pl.when(above < depth)(functools.partial(near_arrived, above))
        if step == 1:
            multiply_right(z)
        else:
            pl.when(below + 1 >= 0)(functools.partial(multiply_right, below + 1))
            pl.when(above - 1 < depth)(functools.partial(multiply_right, above - 1))
    pl.when(z - depth + 1 >= 0)(functools.partial(multiply_right, z - depth + 1))
    pl.when(z + depth - 1 < depth)(functools.partial(multiply_right, z + depth - 1))
    def finish(s, _):
        rows = lax.broadcasted_iota(jnp.int32, (half, width), 0) + core * half
        row_limit = left_dims[me * sectors + s]
        for n in range(coupled):
            j = s * coupled + n
            right = block_right[me * blocks + j]
            owner = right // sectors
            oz, i = owner // 4, (owner % 4) * slots + rank[me, j]
            value = part[core, oz, i] + partner_part[oz, i]
            keep = (rows < row_limit) & (columns[:half] < right_dims[right])
            out[j] = jnp.where(keep, value, 0.0).astype(jnp.bfloat16)
        store(s).start()
        return 0

    def store(s):
        span = pl.ds(s * coupled, coupled)
        return pltpu.make_async_copy(out.at[span], out_hbm.at[span], out_sem.at[s])

    for zz in range(depth):
        swap(zz).wait_recv()
    lax.fori_loop(0, sectors, finish, 0)
    for s in range(sectors):
        store(s).wait()
    for zz in range(depth):
        swap(zz).wait_send()
    for h in (0, 1):
        for zz in range(depth):
            for p in (0, 1):
                to_far(h, zz, p).wait_send()
            for q in range(pieces):
                to_near(h, zz, q).wait_send()
                pl.when((z > 0) & (z <= zz))(lambda: along_z(h, zz, q, False).wait_send())
                pl.when((z < depth - 1) & (z >= zz))(lambda: along_z(h, zz, q, True).wait_send())


def tables(block_right, devices, blocks, sectors):
    slots = blocks // devices
    owners = (block_right // sectors).reshape(devices, blocks)
    position = jnp.arange(blocks, dtype=jnp.int32)
    earlier = (owners[:, None, :] == owners[:, :, None]) & (position[None, None, :] < position[None, :, None])
    rank = jnp.sum(earlier.astype(jnp.int32), axis=2)
    code = owners * slots + rank
    hit = code[:, None, :] == jnp.arange(devices * slots, dtype=jnp.int32)[None, :, None]
    source = jnp.sum(jnp.where(hit, position, 0), axis=2)
    return rank, source


def per_device(psi, left_env, right_env, left_dims, right_dims, block_right):
    devices, cores = lax.axis_size("sector"), lax.axis_size("op")
    blocks, width = psi.shape[0], psi.shape[1]
    terms, sectors = left_env.shape[0], left_env.shape[1]
    if cores != 2 or devices % 4 or terms != 1 or blocks % devices or blocks // devices > sectors:
        return exchange_path(psi, left_env, right_env, left_dims, right_dims, block_right)
    depth, half, slots = devices // 4, width // 2, blocks // devices
    pieces = 2 if sectors % 2 == 0 else 1
    rank, source = tables(block_right, devices, blocks, sectors)
    smem, anywhere = pl.BlockSpec(memory_space=pltpu.SMEM), pl.BlockSpec(memory_space=pl.ANY)
    dma, bf16 = pltpu.SemaphoreType.DMA, jnp.bfloat16
    return pl.pallas_call(
        functools.partial(gather_kernel, devices),
        out_shape=jax.ShapeDtypeStruct((blocks, half, width), bf16),
        in_specs=[smem] * 5 + [anywhere] * 3,
        out_specs=anywhere,
        scratch_shapes=[
            pltpu.VMEM((blocks, half, width), bf16),
            dma((sectors,)),
            pltpu.VMEM((blocks, width, width), bf16),
            pltpu.VMEM((sectors, width, width), bf16),
            pltpu.VMEM((blocks, width, width), bf16),
            pltpu.VMEM((2, depth, 2, sectors, half, width), bf16),
            pltpu.VMEM((2, depth, 2, slots, half, width), bf16),
            pltpu.VMEM((2, depth, 2, slots, half, width), bf16),
            pltpu.VMEM((2, depth, 4 * slots, half, width), jnp.float32),
            pltpu.VMEM((depth, 4 * slots, half, width), jnp.float32),
            dma((2,)),
            dma((2,)),
            dma((2, depth, pieces, 2)),
            dma((2, depth, pieces)),
            dma((2, depth, pieces)),
            dma((2, depth, pieces)),
            dma((2, depth, 2)),
            dma((2, depth, 2)),
            dma((depth,)),
            dma((depth,)),
        ],
        compiler_params=pltpu.CompilerParams(collective_id=0, has_side_effects=True),
    )(block_right, left_dims, right_dims, rank, source, psi, left_env, right_env)


def solution(mesh):
    in_specs = (
        P("sector", None, None),
        P("op", "sector", None, None),
        P("op", "sector", None, None),
        P(),
        P(),
        P(),
    )
    out_specs = P("sector", "op", None)
    return jax.shard_map(
        per_device, mesh=mesh, in_specs=in_specs, out_specs=out_specs, check_vma=False
    )
```

```python
import functools

import jax
import jax.numpy as jnp
from jax import lax
from jax.experimental import pallas as pl
from jax.experimental.pallas import tpu as pltpu
from jax.sharding import PartitionSpec as P

MESH = pl.DeviceIdType.MESH

def combine(partial_sum):
    row_count = partial_sum.shape[1] // lax.axis_size("op")
    whole = lax.psum(partial_sum, "op")
    return lax.dynamic_slice_in_dim(whole, lax.axis_index("op") * row_count, row_count, 1)


def exchange_path(psi, left_env, right_env, left_dims, right_dims, block_right):
    devices = lax.axis_size("sector")
    sector_index = lax.axis_index("sector")
    blocks = psi.shape[0]
    block_width = psi.shape[1]
    term_count = left_env.shape[0]
    sectors = left_env.shape[1]
    coupled = blocks // sectors
    slot_count = blocks // devices
    counter = jnp.arange(blocks, dtype=jnp.int32)
    mine_right = lax.dynamic_slice_in_dim(block_right, sector_index * blocks, blocks)
    mine_owner = mine_right // sectors
    send_order = jnp.argsort(mine_owner * blocks + counter)
    inverse = jnp.argsort(send_order)
    own_dims = lax.dynamic_slice_in_dim(left_dims, sector_index * sectors, sectors)
    row_limit = jnp.repeat(own_dims, coupled)
    col_limit = right_dims[mine_right]
    position = jnp.arange(block_width, dtype=jnp.int32)
    keep_mask = (position[None, :, None] < row_limit[:, None, None]) & (
        position[None, None, :] < col_limit[:, None, None]
    )
    masked = psi * keep_mask.astype(psi.dtype)
    products = jnp.einsum(
        "ksab,snbc->ksnac",
        left_env,
        masked.reshape(sectors, coupled, block_width, block_width),
        preferred_element_type=jnp.float32,
    )
    products = products.astype(jnp.bfloat16).reshape(term_count, blocks, block_width, block_width)
    owners_all = (block_right // sectors).reshape(devices, blocks)
    foreign = (owners_all != sector_index).astype(jnp.int32)
    incoming = jnp.argsort(foreign * blocks + counter[None, :], axis=1)[:, :slot_count]
    arriving = (
        jnp.take_along_axis(block_right.reshape(devices, blocks), incoming, axis=1).reshape(-1)
        - sector_index * sectors
    )
    outgoing = right_env[:, arriving].reshape(
        term_count, devices, slot_count, block_width, block_width
    )
    received = lax.all_to_all(outgoing, "sector", split_axis=1, concat_axis=1, tiled=True)
    chosen = received.reshape(term_count, blocks, block_width, block_width)[:, inverse]
    partial_sum = jnp.einsum("kjab,kjcb->jac", products, chosen, preferred_element_type=jnp.float32)
    result = combine(partial_sum).astype(jnp.bfloat16)
    row_count = result.shape[1]
    op_index = lax.axis_index("op")
    row_position = op_index * row_count + jnp.arange(row_count, dtype=jnp.int32)
    keep_rows = (row_position[None, :, None] < row_limit[:, None, None]) & (
        position[None, None, :] < col_limit[:, None, None]
    )
    return result * keep_rows.astype(jnp.bfloat16)


def gather_kernel(
    devices, block_right, left_dims, right_dims, rank, source, psi_hbm, left_hbm, right_hbm, out_hbm,
    out, out_sem, psi, left, products, full, stage, got, part, partner_part,
    local_sem, own_sem, z_send, z_recv, n_send, n_recv, s_send, s_recv, p_send, p_recv,
):
    me = lax.axis_index("sector")
    core = lax.axis_index("op")
    depth = devices // 4
    z, y, x = me // 4, (me // 2) % 2, me % 2
    x_mate, y_mate = me + 1 - 2 * x, me + 2 - 4 * y
    blocks, width = psi.shape[0], psi.shape[1]
    sectors = left.shape[0]
    coupled = blocks // sectors
    slots = blocks // devices
    half = width // 2
    place = (y, x)
    near = (y_mate, x_mate)
    far = (x_mate, y_mate)

    own = [
        pltpu.make_async_copy(
            right_hbm.at[0, :, pl.ds(h * half, half), :], full.at[h, z, place[h]], own_sem.at[h]
        )
        for h in (0, 1)
    ]
    load_left = pltpu.make_async_copy(left_hbm.at[0], left, local_sem.at[0])
    load_psi = pltpu.make_async_copy(psi_hbm, psi, local_sem.at[1])
    for copy in (*own, load_left, load_psi):
        copy.start()

    barrier = pltpu.get_barrier_semaphore()
    for mate in (x_mate, y_mate):
        pl.semaphore_signal(barrier, inc=1, device_id={"sector": mate}, device_id_type=MESH)
    pl.semaphore_signal(barrier, inc=1, device_id={"op": 1 - core}, device_id_type=MESH)

    @pl.when(z > 0)
    def _():
        pl.semaphore_signal(barrier, inc=1, device_id={"sector": me - 4}, device_id_type=MESH)

    @pl.when(z < depth - 1)
    def _():
        pl.semaphore_signal(barrier, inc=1, device_id={"sector": me + 4}, device_id_type=MESH)

    pl.semaphore_wait(barrier, 3 + (z > 0).astype(jnp.int32) + (z < depth - 1).astype(jnp.int32))
    for copy in own:
        copy.wait()

    def remote(src, dst, send, recv, target):
        return pltpu.make_async_remote_copy(
            src_ref=src, dst_ref=dst, send_sem=send, recv_sem=recv, device_id=target, device_id_type=MESH
        )

    pieces = z_recv.shape[2]
    piece = sectors // pieces

    def along_z(h, zz, q, up):
        block = full.at[h, zz, place[h], pl.ds(q * piece, piece)]
        target = {"sector": me + 4 if up else me - 4}
        return remote(block, block, z_send.at[h, zz, q, int(up)], z_recv.at[h, zz, q], target)

    def to_near(h, zz, q):
        block = full.at[h, zz, place[h], pl.ds(q * piece, piece)]
        return remote(block, block, n_send.at[h, zz, q], n_recv.at[h, zz, q], {"sector": near[h]})

    def to_far(h, zz, p):
        return remote(
            stage.at[h, zz, p], got.at[h, zz, p], s_send.at[h, zz, p], s_recv.at[h, zz, p], {"sector": far[h]}
        )

    def select_and_send(h, zz, p):
        owner = (zz * 2 + p) * 2 + x if h == 0 else (zz * 2 + y) * 2 + p
        for t in range(slots):
            wanted = source[far[h], owner * slots + t] // coupled
            value = full[h, zz, p, 0]
            for s in range(1, sectors):
                value = jnp.where(wanted == s, full[h, zz, p, s], value)
            stage[h, zz, p, t] = value
        to_far(h, zz, p).start()

    def arrived(zz, ups, wait):
        for h in (0, 1):
            for q in range(pieces):
                if wait:
                    along_z(h, zz, q, ups[0]).wait_recv()
                for up in ups:
                    @pl.when(z < depth - 1 if up else z > 0)
                    def _():
                        along_z(h, zz, q, up).start()
                to_near(h, zz, q).start()
            if wait:
                select_and_send(h, zz, place[h])
        if not wait:
            for h in (0, 1):
                select_and_send(h, zz, place[h])

    def near_arrived(zz):
        for h in (0, 1):
            for q in range(pieces):
                to_near(h, zz, q).wait_recv()
            select_and_send(h, zz, 1 - place[h])

    columns = lax.broadcasted_iota(jnp.int32, (width, width), 1)

    def multiply_left(s, _):
        row_limit = left_dims[me * sectors + s]
        env = jnp.where(columns < row_limit, left[s].astype(jnp.float32), 0.0).astype(jnp.bfloat16)
        for n in range(coupled):
            j = s * coupled + n
            col_limit = right_dims[block_right[me * blocks + j]]
            value = jnp.dot(env, psi[j], preferred_element_type=jnp.float32)
            products[j] = jnp.where(columns < col_limit, value, 0.0).astype(jnp.bfloat16)
        return 0

    def swap(zz):
        return remote(
            part.at[1 - core, zz], partner_part.at[zz], p_send.at[zz], p_recv.at[zz], {"op": 1 - core}
        )

    def pick(h, zz, p, wanted, whole):
        if whole:
            return full[h, zz, p, wanted]
        value = full[h, zz, p, 0]
        for s in range(1, sectors):
            value = jnp.where(wanted == s, full[h, zz, p, s], value)
        return value

    def multiply_right(zz, whole=False):
        for h in (0, 1):
            for p in (0, 1):
                to_far(h, zz, p).wait_recv()

        def one(i, _):
            oy, ox, slot = i // (2 * slots), (i // slots) % 2, i % slots
            j = source[me, (zz * 4 + oy * 2 + ox) * slots + slot]
            wanted = j // coupled
            top = jnp.where(ox == x, pick(0, zz, oy, wanted, whole), got[0, zz, oy, slot])
            low = jnp.where(oy == y, pick(1, zz, ox, wanted, whole), got[1, zz, ox, slot])
            env = jnp.concatenate([top, low], axis=0)
            value = lax.dot_general(
                products[j], env, (((1,), (1,)), ((), ())), preferred_element_type=jnp.float32
            )
            part[0, zz, i] = value[:half]
            part[1, zz, i] = value[half:]
            return 0

        lax.fori_loop(0, 4 * slots, one, 0, unroll=4)
        swap(zz).start()

    arrived(z, (False, True), False)
    load_left.wait()
    load_psi.wait()
    lax.fori_loop(0, sectors // 2, multiply_left, 0)
    near_arrived(z)
    for step in range(1, depth):
        below, above = z - step, z + step

        def enter(zz, up):
            arrived(zz, (up,), True)

        pl.when(below >= 0)(functools.partial(enter, below, True))
        pl.when(above < depth)(functools.partial(enter, above, False))
        if step == 1:
            lax.fori_loop(sectors // 2, sectors, multiply_left, 0)
        pl.when(below >= 0)(functools.partial(near_arrived, below))
        pl.when(above < depth)(functools.partial(near_arrived, above))
        if step == 1:
            multiply_right(z)
        else:
            pl.when(below + 1 >= 0)(functools.partial(multiply_right, below + 1))
            pl.when(above - 1 < depth)(functools.partial(multiply_right, above - 1))
    pl.when(z - depth + 1 >= 0)(functools.partial(multiply_right, z - depth + 1, True))
    pl.when(z + depth - 1 < depth)(functools.partial(multiply_right, z + depth - 1, True))
    def finish(s, _):
        rows = lax.broadcasted_iota(jnp.int32, (half, width), 0) + core * half
        row_limit = left_dims[me * sectors + s]
        for n in range(coupled):
            j = s * coupled + n
            right = block_right[me * blocks + j]
            owner = right // sectors
            oz, i = owner // 4, (owner % 4) * slots + rank[me, j]
            value = part[core, oz, i] + partner_part[oz, i]
            keep = (rows < row_limit) & (columns[:half] < right_dims[right])
            out[j] = jnp.where(keep, value, 0.0).astype(jnp.bfloat16)
        store(s).start()
        return 0

    def store(s):
        span = pl.ds(s * coupled, coupled)
        return pltpu.make_async_copy(out.at[span], out_hbm.at[span], out_sem.at[s])

    for zz in range(depth):
        swap(zz).wait_recv()
    lax.fori_loop(0, sectors, finish, 0)
    for s in range(sectors):
        store(s).wait()
    for zz in range(depth):
        swap(zz).wait_send()
    for h in (0, 1):
        for zz in range(depth):
            for p in (0, 1):
                to_far(h, zz, p).wait_send()
            for q in range(pieces):
                to_near(h, zz, q).wait_send()
                pl.when((z > 0) & (z <= zz))(lambda: along_z(h, zz, q, False).wait_send())
                pl.when((z < depth - 1) & (z >= zz))(lambda: along_z(h, zz, q, True).wait_send())


def tables(block_right, devices, blocks, sectors):
    slots = blocks // devices
    owners = (block_right // sectors).reshape(devices, blocks)
    position = jnp.arange(blocks, dtype=jnp.int32)
    earlier = (owners[:, None, :] == owners[:, :, None]) & (position[None, None, :] < position[None, :, None])
    rank = jnp.sum(earlier.astype(jnp.int32), axis=2)
    code = owners * slots + rank
    hit = code[:, None, :] == jnp.arange(devices * slots, dtype=jnp.int32)[None, :, None]
    source = jnp.sum(jnp.where(hit, position, 0), axis=2)
    return rank, source


def per_device(psi, left_env, right_env, left_dims, right_dims, block_right):
    devices, cores = lax.axis_size("sector"), lax.axis_size("op")
    blocks, width = psi.shape[0], psi.shape[1]
    terms, sectors = left_env.shape[0], left_env.shape[1]
    if cores != 2 or devices % 4 or terms != 1 or blocks % devices or blocks // devices > sectors:
        return exchange_path(psi, left_env, right_env, left_dims, right_dims, block_right)
    depth, half, slots = devices // 4, width // 2, blocks // devices
    pieces = 2 if sectors % 2 == 0 else 1
    rank, source = tables(block_right, devices, blocks, sectors)
    smem, anywhere = pl.BlockSpec(memory_space=pltpu.SMEM), pl.BlockSpec(memory_space=pl.ANY)
    dma, bf16 = pltpu.SemaphoreType.DMA, jnp.bfloat16
    return pl.pallas_call(
        functools.partial(gather_kernel, devices),
        out_shape=jax.ShapeDtypeStruct((blocks, half, width), bf16),
        in_specs=[smem] * 5 + [anywhere] * 3,
        out_specs=anywhere,
        scratch_shapes=[
            pltpu.VMEM((blocks, half, width), bf16),
            dma((sectors,)),
            pltpu.VMEM((blocks, width, width), bf16),
            pltpu.VMEM((sectors, width, width), bf16),
            pltpu.VMEM((blocks, width, width), bf16),
            pltpu.VMEM((2, depth, 2, sectors, half, width), bf16),
            pltpu.VMEM((2, depth, 2, slots, half, width), bf16),
            pltpu.VMEM((2, depth, 2, slots, half, width), bf16),
            pltpu.VMEM((2, depth, 4 * slots, half, width), jnp.float32),
            pltpu.VMEM((depth, 4 * slots, half, width), jnp.float32),
            dma((2,)),
            dma((2,)),
            dma((2, depth, pieces, 2)),
            dma((2, depth, pieces)),
            dma((2, depth, pieces)),
            dma((2, depth, pieces)),
            dma((2, depth, 2)),
            dma((2, depth, 2)),
            dma((depth,)),
            dma((depth,)),
        ],
        compiler_params=pltpu.CompilerParams(collective_id=0, has_side_effects=True),
    )(block_right, left_dims, right_dims, rank, source, psi, left_env, right_env)


def solution(mesh):
    in_specs = (
        P("sector", None, None),
        P("op", "sector", None, None),
        P("op", "sector", None, None),
        P(),
        P(),
        P(),
    )
    out_specs = P("sector", "op", None)
    return jax.shard_map(
        per_device, mesh=mesh, in_specs=in_specs, out_specs=out_specs, check_vma=False
    )
```
